128 devices in a mesh: node: 32 (over z, x, core), mp: 4 (over y).
Axes of the slice: x: 4, y: 4, z: 4, core: 2. Of those that a mesh axis runs over, the one named last changes fastest.
Arguments:
- queries: bfloat16 [128, 64, 128], P('node', 'mp'), may hold values from -8 to 8
- root_keys: bfloat16 [16384, 8, 128], P('node', 'mp'), may hold values from -6 to 6
- root_values: bfloat16 [16384, 8, 128], P('node', 'mp'), may hold values from -6 to 6
- mid_keys: bfloat16 [32, 1024, 8, 128], P('node', None, 'mp'), may hold values from -6 to 6
- mid_values: bfloat16 [32, 1024, 8, 128], P('node', None, 'mp'), may hold values from -6 to 6
- leaf_keys: bfloat16 [128, 256, 8, 128], P('node', None, 'mp'), may hold values from -6 to 6
- leaf_values: bfloat16 [128, 256, 8, 128], P('node', None, 'mp'), may hold values from -6 to 6
- mid_length: int32 [32], replicated, may hold values from 1 to 1024
- leaf_length: int32 [128], P('node'), may hold values from 1 to 256
- branch_mid: int32 [128, 1], replicated, may hold values from 0 to 31; in each aligned block of 128 rows (0 to 127, 128 to 255, ...) at most 8 rows name the same one
- residual: bfloat16 [128, 8192], P(None, 'node'), may hold values from -6 to 6
- norm_gain: float32 [8192], P('node'), may hold values from 0.5 to 1.5
- out_weight: bfloat16 [8192, 8192], P('mp', 'node'), may hold values from -0.0625 to 0.0625
- gate_weight: bfloat16 [8192, 28672], P('node', 'mp'), may hold values from -0.0625 to 0.0625
- up_weight: bfloat16 [8192, 28672], P('node', 'mp'), may hold values from -0.0625 to 0.0625
- down_weight: bfloat16 [28672, 8192], P('mp', 'node'), may hold values from -0.03125 to 0.03125
Outputs:
- layer_out: bfloat16 [128, 8192], P('mp', 'node')
The draws below stay inside these ranges and needn't reach their ends.
Inputs may be any that keep to these rules, and one draw needn't show every extreme that they name: `branch_mid`: every inner tree node lies on the path of 1 to 8 branches, and some node on exactly 8.
All inputs are finite; a program needn't handle non-finite values.
Results may differ from the reference program's by a relative error of at most 0.015.
Values may be sent and summed in bfloat16 or wider, within the bound.
No kernel may reach another device: no remote copies, remote signals or barrier semaphores. Data moves between devices by JAX's collectives and lax.ppermute only.
A program may use at most 64 MiB of HBM per device.

```python
import math
import jax
import jax.numpy as jnp
import numpy as np
from jax import lax

D = 8192
FF = 28672
QH = 64
KVH = 8
HD = 128
MID_LEN = 1024
LEAF = 256
ROOT = 16384
CAP = 8
BRANCHES = 128
MIDS = 32


def draw_queries(key, part):
    values = jnp.clip(jax.random.normal(jax.random.fold_in(key, 5), (BRANCHES, QH, HD), jnp.float32), -6.0, 6.0)
    return values.astype(jnp.bfloat16)


def draw_root_keys(key, part):
    values = jnp.clip(jax.random.normal(jax.random.fold_in(key, 9), (ROOT, KVH, HD), jnp.float32), -6.0, 6.0)
    return values.astype(jnp.bfloat16)


def touch_ends(values, own_key, smallest, largest):
    dims = values.shape
    place = [jax.random.randint(jax.random.fold_in(own_key, axis), (), 0, dims[axis]) for axis in range(len(dims))]
    values = values.at[tuple(place)].set(smallest)
    longest = dims.index(max(dims))
    place[longest] = (place[longest] + 1) % dims[longest]
    return values.at[tuple(place)].set(largest)


def block_scale(key, shape, split, low, largest):
    factor_of, own = 1.0, jax.random.fold_in(key, 6)
    for position, shards_of in split:
        draws = jnp.exp(jax.random.uniform(jax.random.fold_in(own, position), (shards_of,), jnp.float32, low / len(split), largest / len(split)))
        factor_of = factor_of * jnp.repeat(draws, shape[position] // shards_of).reshape([-1 if axis == position else 1 for axis in range(len(shape))])
    return factor_of


def assign_block(own_key, own, number, rows, number_of, top, limit, lean):
    ranking = jax.random.permutation(own_key, number_of)
    crowded, common = load_shares(number_of, rows * top, limit, lean, True), load_shares(number_of, rows * top, limit, lean, False)
    places = jnp.arange(number_of)

    def named(sizes, offset_by):
        used = int((sizes > 0).sum())
        fixed = max(1, used // 4)
        moved = fixed + (places - fixed + offset_by * (used - fixed)) % max(1, number_of - fixed)
        return jnp.zeros((number_of,), jnp.int32).at[ranking[jnp.where(places < fixed, places, moved)]].set(jnp.asarray(sizes, jnp.int32))

    sizes = jnp.where(number % 4 == 0, named(crowded, number // 4), named(common, number - number // 4 - 1))
    mixed = jax.random.permutation(jax.random.fold_in(own, 3), number_of)
    source_of, taker = mixed[0:number_of // 2 * 2:2], mixed[1:number_of // 2 * 2:2]
    slack = jnp.minimum(sizes[source_of] - 1, limit - sizes[taker]) // 2
    slack = jnp.where((source_of == ranking[0]) | (taker == ranking[0]) | (sizes[taker] == 0), 0, jnp.maximum(slack, 0))
    moved = jax.random.randint(jax.random.fold_in(own, 4), (number_of // 2,), 0, 1 << 20) % (slack + 1)
    sizes = sizes.at[source_of].add(-moved).at[taker].add(moved)
    labels = jnp.searchsorted(jnp.cumsum(sizes), jnp.arange(rows * top), side="right").astype(jnp.int32)
    grid = labels.reshape(top, rows).T
    grid = grid[jax.random.permutation(jax.random.fold_in(own, 1), rows)]
    offset_by = jax.random.randint(jax.random.fold_in(own, 2), (rows, 1), 0, top)
    return jnp.take_along_axis(grid, (jnp.arange(top)[None, :] + offset_by) % top, axis=1)


def load_shares(amount, total, limit, skew, full):
    portions = [(1 << 20) // math.isqrt(standing ** skew) + 1 for standing in range(1, amount + 1)]
    largest = limit if full else min(limit, max(-(-total // amount), total * portions[0] // sum(portions)))
    least = 1 if total - largest >= amount - 1 else 0
    counts, rest = [largest] + [least] * (amount - 1), total - largest - least * (amount - 1)
    while rest > 0:
        movable = [i for i in range(1, amount) if counts[i] < largest] or [i for i in range(1, amount) if counts[i] < limit]
        mass, budget = sum([portions[i] for i in movable]), rest
        for i in movable:
            addition = min(limit - counts[i], max(1, budget * portions[i] // mass), rest)
            counts[i] = counts[i] + addition
            rest = rest - addition
    return np.array(counts)


def scatter_about(key, dims, deviation, most, pieces=(), held_as=jnp.bfloat16):
    drawn = deviation * jax.random.normal(key, dims, jnp.float32)
    if pieces:
        drawn = drawn * block_scale(key, dims, pieces, -0.22, 0.18)
    return jnp.clip(drawn, -most, most).astype(held_as)


def setup_inputs(seed: int = 0) -> dict:
    key_of = jax.random.split(jax.random.key(seed), 17)
    queries = draw_queries(jax.random.fold_in(key_of[16], 71), 0)
    root_keys = draw_root_keys(jax.random.fold_in(key_of[16], 71), 0)
    root_values = scatter_about(key_of[2], (ROOT, KVH, HD), 1.0, 6.0, ((0, 32), (1, 4)))
    mid_keys = scatter_about(key_of[3], (MIDS, MID_LEN, KVH, HD), 1.0, 6.0, ((0, 32), (2, 4)))
    mid_values = scatter_about(key_of[4], (MIDS, MID_LEN, KVH, HD), 1.0, 6.0, ((0, 32), (2, 4)))
    leaf_keys = scatter_about(key_of[5], (BRANCHES, LEAF, KVH, HD), 1.0, 6.0, ((0, 32), (2, 4)))
    leaf_values = scatter_about(key_of[6], (BRANCHES, LEAF, KVH, HD), 1.0, 6.0, ((0, 32), (2, 4)))
    mid_length = touch_ends(jax.random.randint(key_of[7], (MIDS,), 1, MID_LEN + 1), jax.random.fold_in(key_of[7], 1), 1, MID_LEN).astype(jnp.int32)
    leaf_length = touch_ends(jax.random.randint(key_of[8], (BRANCHES,), 1, LEAF + 1), jax.random.fold_in(key_of[8], 1), 1, LEAF).astype(jnp.int32)
    branch_mid_keys = jax.random.split(jax.random.fold_in(key_of[9], 1), BRANCHES // BRANCHES)
    branch_mid_turns = jax.random.permutation(jax.random.fold_in(key_of[9], 3), BRANCHES // BRANCHES)
    branch_mid = jax.vmap(lambda own, number: assign_block(jax.random.fold_in(key_of[9], 2), own, number, BRANCHES, MIDS, 1, CAP, 2))(branch_mid_keys, branch_mid_turns).reshape((BRANCHES, 1))
    residual = scatter_about(key_of[10], (BRANCHES, D), 1.0, 6.0, ((1, 32),))
    norm_gain = jnp.clip(1.0 + 0.1 * jax.random.normal(key_of[11], (D,), jnp.float32), 0.5, 1.5)
    out_weight = scatter_about(key_of[12], (QH * HD, D), (QH * HD) ** -0.5, 0.0625, ((0, 4), (1, 32)))
    gate_weight = scatter_about(key_of[13], (D, FF), D ** -0.5, 0.0625, ((0, 32), (1, 4)))
    up_weight = scatter_about(key_of[14], (D, FF), D ** -0.5, 0.0625, ((0, 32), (1, 4)))
    down_weight = scatter_about(key_of[15], (FF, D), FF ** -0.5, 0.03125, ((0, 4), (1, 32)))
    return dict(queries=queries, root_keys=root_keys, root_values=root_values, mid_keys=mid_keys, mid_values=mid_values, leaf_keys=leaf_keys, leaf_values=leaf_values, mid_length=mid_length, leaf_length=leaf_length, branch_mid=branch_mid, residual=residual, norm_gain=norm_gain, out_weight=out_weight, gate_weight=gate_weight, up_weight=up_weight, down_weight=down_weight)


masked_score = -1e+30
norm_eps = 1e-05

def reference(queries, root_keys, root_values, mid_keys, mid_values, leaf_keys, leaf_values, mid_length, leaf_length, branch_mid, residual, norm_gain, out_weight, gate_weight, up_weight, down_weight):
    group_size = QH // KVH
    scaling = 1.0 / math.sqrt(HD)

    def attend(inputs):
        query_rows, mid_index, leaf_key, leaf_value, leaf_count = inputs
        key_block = jnp.concatenate([root_keys, mid_keys[mid_index], leaf_key], axis=0).astype(jnp.float32)
        value_block = jnp.concatenate([root_values, mid_values[mid_index], leaf_value], axis=0).astype(jnp.float32)
        mid_count = mid_length[mid_index]
        usable = jnp.concatenate([jnp.ones((ROOT,), dtype=bool), jnp.arange(MID_LEN) < mid_count, jnp.arange(LEAF) < leaf_count])
        grouped = query_rows.astype(jnp.float32).reshape(KVH, group_size, HD)
        scores = jnp.einsum('kgd,lkd->kgl', grouped, key_block, precision=lax.Precision.HIGHEST) * scaling
        scores = jnp.where(usable, scores, masked_score)
        highest = lax.optimization_barrier(jnp.max(scores, axis=-1, keepdims=True))
        weights = jnp.where(usable, jnp.exp(scores - highest), 0.0)
        rounded = weights.astype(jnp.bfloat16).astype(jnp.float32)
        weighted = jnp.einsum('kgl,lkd->kgd', rounded, value_block, precision=lax.Precision.HIGHEST)
        return (weighted / lax.optimization_barrier(jnp.sum(weights, axis=-1))[..., None]).reshape(QH * HD)
    attended = lax.map(attend, (queries, branch_mid[:, 0], leaf_keys, leaf_values, leaf_length)).astype(jnp.bfloat16)
    stream = residual.astype(jnp.float32) + jnp.dot(attended, out_weight, preferred_element_type=jnp.float32)
    mean_square = lax.optimization_barrier(jnp.sum(stream * stream, axis=1, keepdims=True)) / D
    normed = (stream * lax.rsqrt(mean_square + norm_eps) * norm_gain[None, :]).astype(jnp.bfloat16)
    gate = jnp.dot(normed, gate_weight, preferred_element_type=jnp.float32)
    upward = jnp.dot(normed, up_weight, preferred_element_type=jnp.float32)
    act = (jax.nn.silu(gate) * upward).astype(jnp.bfloat16)
    return (stream + jnp.dot(act, down_weight, preferred_element_type=jnp.float32)).astype(jnp.bfloat16)
```

```python
import jax
import jax.numpy as jnp
from jax import lax
from jax.sharding import Mesh
from jax.sharding import PartitionSpec as P

D = 8192
CAP = 8
masked_score = -1e30
norm_eps = 1e-05
bf16 = jnp.bfloat16
f32 = jnp.float32
PLANE = ("z", "x")
NODE = ("z", "x", "core")
SWAP = [(0, 1), (1, 0)]


def exchange(x, axes):
    return lax.all_to_all(x, axes, split_axis=0, concat_axis=0, tiled=True)


def swapped(x):
    return lax.ppermute(x, "core", SWAP)


def rounded(x):
    return lax.reduce_precision(x, 8, 7)


def in_pieces(x):
    first = rounded(x)
    second = rounded(x - first)
    third = x - first - second
    return first.astype(bf16), second.astype(bf16), third.astype(bf16)


def attend(queries, keys, values, usable, scaling):
    scores = jnp.einsum("...qd,...ld->...ql", queries, keys, preferred_element_type=f32) * scaling
    scores = jnp.where(usable, scores, masked_score)
    highest = jnp.max(scores, axis=-1, keepdims=True)
    weights = jnp.where(usable, jnp.exp(scores - highest), 0.0)
    weighted = jnp.einsum(
        "...ql,...ld->...qd", weights.astype(bf16), values, preferred_element_type=f32
    )
    return highest, jnp.sum(weights, axis=-1, keepdims=True), weighted


def on_device(
    queries,
    root_keys,
    root_values,
    mid_keys,
    mid_values,
    leaf_keys,
    leaf_values,
    mid_length,
    leaf_length,
    branch_mid,
    residual,
    norm_gain,
    out_weight,
    gate_weight,
    up_weight,
    down_weight,
):
    core = lax.axis_index("core")
    other = 1 - core
    chip = lax.axis_index(PLANE)
    head_size = queries.shape[2]
    group = queries.shape[1] // 2
    scaling = head_size ** (-0.5)
    chips = 16

    halves = queries.reshape(4, 2, group, head_size).transpose(1, 0, 2, 3)
    sent = jnp.broadcast_to(halves[None], (chips, *halves.shape)).reshape(32, 4, group, head_size)
    gathered = exchange(sent, NODE).reshape(128, group, head_size)

    caches = (root_keys, root_values, mid_keys, mid_values, leaf_keys, leaf_values)

    def of_head(x, head):
        return lax.dynamic_index_in_dim(x, head, x.ndim - 2, keepdims=False).reshape(-1, head_size)

    kept = jnp.concatenate([of_head(x, core) for x in caches])
    arrived = swapped(jnp.concatenate([of_head(x, other) for x in caches]))
    spans, at = [], 0
    for x in caches:
        rows = x.size // 2 // head_size
        spans.append((at, at + rows))
        at += rows
    pair = [(kept[a:b], arrived[a:b]) for a, b in spans]
    lengths = (leaf_length, swapped(leaf_length))

    def ordered(a, b):
        return jnp.where(core == 0, jnp.stack([a, b]), jnp.stack([b, a]))

    hidden = gate_weight.shape[1] // 2

    def columns(w, half):
        return lax.dynamic_slice_in_dim(w, half * hidden, hidden, 1)

    def rows_of(w, half):
        return lax.dynamic_slice_in_dim(w, half * hidden, hidden, 0)

    gate_far = swapped(columns(gate_weight, other))
    up_far = swapped(columns(up_weight, other))
    down_far = swapped(rows_of(down_weight, other))
    gain_far = swapped(norm_gain)

    flat = gathered.reshape(128 * group, head_size)
    root_high, root_total, root_weighted = attend(
        flat, jnp.concatenate(pair[0]), jnp.concatenate(pair[1]), True, scaling
    )
    nodes = jnp.stack([2 * chip + core, 2 * chip + other])
    routing = branch_mid[:, 0]
    place = jnp.arange(128)
    earlier = (routing[None, :] == routing[:, None]) & (place[None, :] < place[:, None])
    rank = jnp.sum(earlier.astype(jnp.int32), axis=1)
    chosen = (routing[None, None, :] == nodes[:, None, None]) & (
        rank[None, None, :] == jnp.arange(CAP)[None, :, None]
    )
    picked = jnp.einsum(
        "ncb,bgd->ncgd", chosen.astype(bf16), gathered, preferred_element_type=f32
    ).astype(bf16)
    usable = jnp.arange(mid_keys.shape[1])[None, None, :] < mid_length[nodes][:, None, None]
    mid_high, mid_total, mid_weighted = attend(
        picked.reshape(2, CAP * group, head_size),
        jnp.stack(pair[2]),
        jnp.stack(pair[3]),
        usable,
        scaling,
    )
    exact = lax.Precision.HIGHEST
    spread = chosen.astype(f32)
    mid_all = jnp.concatenate([mid_weighted, mid_high, mid_total], axis=-1).reshape(2, CAP, group, -1)
    back = jnp.einsum("ncb,ncgd->bgd", spread, mid_all, precision=exact).reshape(128 * group, -1)
    covered = jnp.sum(spread, axis=(0, 1))
    lack = jnp.repeat((1.0 - covered) * masked_score, group)[:, None]
    back_weighted = back[:, :head_size]
    back_high = back[:, head_size : head_size + 1] + lack
    back_total = back[:, head_size + 1 :]
    high = jnp.maximum(root_high, back_high)
    root_factor = jnp.exp(root_high - high)
    back_factor = jnp.exp(back_high - high)
    total = root_total * root_factor + back_total * back_factor
    mean = (root_weighted * root_factor + back_weighted * back_factor) / total
    level = (high + jnp.log(total)).reshape(chips, -1)
    first, second, third = in_pieces(level)
    stats = jnp.stack(
        [
            jnp.concatenate([first, second], axis=1),
            jnp.concatenate([third, jnp.zeros_like(third)], axis=1),
        ],
        axis=1,
    )
    payload = jnp.concatenate([mean.astype(bf16).reshape(chips, 64, head_size), stats], axis=1)
    parts = exchange(payload, PLANE)
    means = parts[:, :64].astype(f32)
    stats = parts[:, 64:].astype(f32)
    level = stats[:, 0, :64] + stats[:, 0, 64:] + stats[:, 1, :64]
    mine = ordered(halves_of(queries, core, group), swapped(halves_of(queries, other, group)))
    leaf_usable = (
        jnp.arange(leaf_keys.shape[1])[None, None, :]
        < ordered(*lengths).reshape(8)[:, None, None]
    )
    leaf_high, leaf_total, leaf_weighted = attend(
        mine.reshape(8, group, head_size),
        ordered(*pair[4]).reshape(8, -1, head_size),
        ordered(*pair[5]).reshape(8, -1, head_size),
        leaf_usable,
        scaling,
    )
    leaf_high = leaf_high.reshape(64)
    high = jnp.maximum(jnp.max(level, axis=0), leaf_high)
    factor = jnp.exp(level - high[None])
    leaf_factor = jnp.exp(leaf_high - high)
    total = jnp.sum(factor, axis=0) + leaf_factor * leaf_total.reshape(64)
    weighted = jnp.sum(means * factor[:, :, None], axis=0) + leaf_factor[:, None] * leaf_weighted.reshape(64, head_size)
    attended = (weighted / total[:, None]).astype(bf16).reshape(8, group * head_size)

    near = exchange(jnp.broadcast_to(attended[None], (chips, *attended.shape)), PLANE)
    near = near.reshape(128, group * head_size)
    far = swapped(near)
    half_rows = out_weight.shape[0] // 2
    projected = jnp.dot(
        near, lax.dynamic_slice_in_dim(out_weight, core * half_rows, half_rows, 0), preferred_element_type=f32
    ) + jnp.dot(
        far, lax.dynamic_slice_in_dim(out_weight, other * half_rows, half_rows, 0), preferred_element_type=f32
    )
    shares = exchange(jnp.broadcast_to(projected.astype(bf16)[None], (4, *projected.shape)), "mp")
    stream = residual.astype(f32) + jnp.sum(shares.astype(f32), axis=0)
    stream_far = swapped(stream)
    squares = jnp.sum(stream * stream, axis=1) + jnp.sum(stream_far * stream_far, axis=1)
    scaled = (stream * norm_gain[None]).astype(bf16)
    scaled_far = (stream_far * gain_far[None]).astype(bf16)

    def both(w, far):
        return (
            jnp.dot(scaled, columns(w, core), preferred_element_type=f32)
            + jnp.dot(scaled_far, far, preferred_element_type=f32)
        ).astype(bf16)

    pieces = jnp.stack(in_pieces(squares), axis=1)
    pieces = jnp.pad(pieces, ((0, 0), (0, 125)))
    payload = jnp.concatenate([both(gate_weight, gate_far), both(up_weight, up_far), pieces], axis=1)
    parts = exchange(payload.reshape(chips, 8, -1), PLANE)
    summed = jnp.sum(parts.astype(f32), axis=0)
    inverse = lax.rsqrt(jnp.sum(summed[:, 2 * hidden : 2 * hidden + 3], axis=1, keepdims=True) / D + norm_eps)
    gate = summed[:, :hidden] * inverse
    upward = summed[:, hidden : 2 * hidden] * inverse
    act = (jax.nn.silu(gate) * upward).astype(bf16)
    acts = exchange(jnp.broadcast_to(act[None], (chips, *act.shape)), PLANE).reshape(128, hidden)
    own = jnp.dot(acts, rows_of(down_weight, core), preferred_element_type=f32).astype(bf16)
    partner = jnp.dot(acts, down_far, preferred_element_type=f32).astype(bf16)
    blocks = ordered(own, partner).reshape(8, 32, -1)
    arrived = exchange(blocks, ("core", "mp"))
    rows = lax.dynamic_slice_in_dim(stream, lax.axis_index("mp") * 32, 32, 0)
    return (rows + jnp.sum(arrived.astype(f32), axis=0)).astype(bf16)


def halves_of(queries, half, group):
    return lax.dynamic_slice_in_dim(queries, half * group, group, 1)


def solution(mesh):
    fine = Mesh(mesh.devices.reshape(4, 4, 2, 4), ("z", "x", "core", "mp"))
    in_specs = (
        P(NODE, "mp", None),
        P(NODE, "mp", None),
        P(NODE, "mp", None),
        P(NODE, None, "mp", None),
        P(NODE, None, "mp", None),
        P(NODE, None, "mp", None),
        P(NODE, None, "mp", None),
        P(),
        P(NODE),
        P(),
        P(None, NODE),
        P(NODE),
        P("mp", NODE),
        P(NODE, "mp"),
        P(NODE, "mp"),
        P("mp", NODE),
    )
    return jax.shard_map(
        on_device, mesh=fine, in_specs=in_specs, out_specs=P("mp", NODE), check_vma=False
    )
```

```python
import functools
import math

import jax
import jax.numpy as jnp
from jax import lax
from jax.experimental import pallas as pl
from jax.experimental.pallas import tpu as pltpu
from jax.sharding import Mesh
from jax.sharding import PartitionSpec as P

D = 8192
CAP = 8
masked_score = -1e30
norm_eps = 1e-05
bf16 = jnp.bfloat16
f32 = jnp.float32
PLANE = ("z", "x")
NODE = ("z", "x", "core")
SWAP = [(0, 1), (1, 0)]


def exchange(x, axes):
    return lax.all_to_all(x, axes, split_axis=0, concat_axis=0, tiled=True)


def swapped(x):
    return lax.ppermute(x, "core", SWAP)


VMEM = pl.BlockSpec(memory_space=pltpu.VMEM)
SMEM = pl.BlockSpec(memory_space=pltpu.SMEM)
HBM = pl.BlockSpec(memory_space=pltpu.HBM)
CHIPS = 16
HEADS = 8
LEVEL = 128**-0.5 * math.log2(math.e)


def dot_rows(a, b):
    return lax.dot_general(a, b, (((1,), (1,)), ((), ())), preferred_element_type=f32)


def dot(a, b):
    return lax.dot_general(a, b, (((1,), (0,)), ((), ())), preferred_element_type=f32)


def iota(shape, dim):
    return lax.broadcasted_iota(jnp.int32, shape, dim)


def cut_kernel(core, after, gate, up, down, pair_ref, down_ref, sems):
    rows, hidden = gate.shape[0], down_ref.shape[0]
    half = pl.ds(pl.multiple_of((1 - core[0]) * hidden, 512), hidden)
    copies = [
        pltpu.make_async_copy(gate.at[:, half], pair_ref.at[0:rows], sems.at[0]),
        pltpu.make_async_copy(up.at[:, half], pair_ref.at[rows : 2 * rows], sems.at[1]),
        pltpu.make_async_copy(down.at[half, :], down_ref, sems.at[2]),
    ]
    for copy in copies:
        copy.start()
    for copy in copies:
        copy.wait()


def cut(core, after, gate, up, down):
    hidden = gate.shape[1] // 2
    return pl.pallas_call(
        cut_kernel,
        out_shape=(
            jax.ShapeDtypeStruct((2 * gate.shape[0], hidden), bf16),
            jax.ShapeDtypeStruct((hidden, down.shape[1]), bf16),
        ),
        in_specs=[SMEM] + [HBM] * 4,
        out_specs=(VMEM, VMEM),
        scratch_shapes=[pltpu.SemaphoreType.DMA((3,))],
        compiler_params=pltpu.CompilerParams(vmem_limit_bytes=56 << 20),
        cost_estimate=pl.CostEstimate(flops=0, bytes_accessed=11_000_000, transcendentals=0),
        name="cut",
    )(core, after, gate, up, down)


def split_kernel(core, *refs):
    sources, out_ref = refs[:4], refs[4]
    order = jnp.where(2 * iota((128, 256), 0) + core[0] == iota((128, 256), 1), 1.0, 0.0).astype(bf16)
    for i, ref in enumerate(sources):
        for start in range(0, ref.shape[0], 512):
            pair = jnp.concatenate([ref[start : start + 256], ref[start + 256 : start + 512]], axis=1)
            moved = dot(order, pair).astype(bf16)
            out_ref[i, start // 2 : start // 2 + 128] = moved[:, 0:128]
            out_ref[i, start // 2 + 128 : start // 2 + 256] = moved[:, 128:256]


def split_root(core, roots):
    sources = [flat(x) for x in roots]
    return pl.pallas_call(
        split_kernel,
        out_shape=jax.ShapeDtypeStruct((4, sources[0].shape[0] // 2, 128), bf16),
        in_specs=[SMEM] + [VMEM] * 4,
        out_specs=VMEM,
        compiler_params=pltpu.CompilerParams(vmem_limit_bytes=16 << 20),
        cost_estimate=pl.CostEstimate(flops=70_000_000, bytes_accessed=1_600_000, transcendentals=0),
        name="split_root",
    )(core, *sources)


def shared_kernel(scalars, q_ref, column_ref, row_ref, *refs):
    mids, (split, out_ref) = refs[:4], refs[4:]
    core = scalars[0]
    count = q_ref.shape[0]
    queries = q_ref[...]
    one = jnp.where(row_ref[...] == iota((128, count), 0), 1.0, 0.0).astype(bf16)
    picked = dot(one, queries).astype(bf16)
    levels, means = [], []
    for i in range(2):
        scores = dot_rows(picked[64 * i : 64 * i + 64], mids[2 * i][...])
        lane = iota(scores.shape, 1)
        usable = (lane % 2 == core) & (lane < 2 * scalars[1 + i])
        scores = jnp.where(usable, scores, masked_score)
        highest = jnp.max(scores, axis=1, keepdims=True)
        weights = jnp.where(usable, jnp.exp2((scores - highest) * LEVEL), 0.0)
        total = jnp.sum(weights, axis=1, keepdims=True)
        weighted = dot(weights.astype(bf16), mids[2 * i + 1][...])
        levels.append(highest * LEVEL + jnp.log2(total))
        means.append(weighted / total)
    level = jnp.concatenate(levels)
    mean = jnp.concatenate(means)
    eye = iota((128, 128), 0) == iota((128, 128), 1)
    level_row = jnp.sum(jnp.where(eye, level, 0.0), axis=0, keepdims=True)
    first = mean.astype(bf16)
    second = (mean - first.astype(f32)).astype(bf16)
    step = 256
    lanes = iota((64, 128), 1)
    diagonal = (lanes % 64) == iota((64, 128), 0)
    for at in range(0, count, step):
        here = column_ref[at : at + step] == iota((step, 128), 1)
        chosen = jnp.where(here, 1.0, 0.0).astype(bf16)
        known = dot(chosen, first) + dot(chosen, second)
        known_level = jnp.max(jnp.where(here, level_row, masked_score), axis=1, keepdims=True)
        rows = q_ref[at : at + step]
        near = dot_rows(rows, split[0])
        far = dot_rows(rows, split[2])
        highest = jnp.maximum(
            jnp.max(near, axis=1, keepdims=True), jnp.max(far, axis=1, keepdims=True)
        )
        top = jnp.maximum(highest * LEVEL, known_level)
        near = jnp.exp2(near * LEVEL - top)
        far = jnp.exp2(far * LEVEL - top)
        factor = jnp.exp2(known_level - top)
        total = factor + jnp.sum(near, axis=1, keepdims=True) + jnp.sum(far, axis=1, keepdims=True)
        weighted = (
            known * factor
            + dot(near.astype(bf16), split[1])
            + dot(far.astype(bf16), split[3])
        )
        result = weighted / total
        reached = top + jnp.log2(total)
        for j in range(step // 64):
            chip = at // 64 + j
            out_ref[chip, 0:64] = result[64 * j : 64 * j + 64].astype(bf16)
            line = jnp.sum(
                jnp.where(diagonal, reached[64 * j : 64 * j + 64], 0.0), axis=0, keepdims=True
            )
            large = line.astype(bf16).astype(f32)
            middle = (line - large).astype(bf16).astype(f32)
            small = line - large - middle
            pair = jnp.where(iota((1, 128), 1) < 64, large, middle)
            both = jnp.where(iota((16, 128), 0) == 0, pair, small)
            out_ref[chip, 64:80] = both.astype(bf16)


def flat(x):
    return x.reshape(-1, 128)


def shared_part(scalars, queries, column, row, mids, roots):
    return pl.pallas_call(
        shared_kernel,
        out_shape=jax.ShapeDtypeStruct((CHIPS, 80, 128), bf16),
        in_specs=[SMEM] + [VMEM] * 8,
        out_specs=VMEM,
        compiler_params=pltpu.CompilerParams(vmem_limit_bytes=32 << 20),
        cost_estimate=pl.CostEstimate(flops=800_000_000, bytes_accessed=4_300_000, transcendentals=1_200_000),
        name="shared_part",
    )(scalars, queries, column, row, *[flat(x) for x in mids], roots)


def own_kernel(scalars, q_ref, *refs):
    held, (high_ref, total_ref, mean_ref) = refs[:4], refs[4:]
    core, chip = scalars[0], scalars[1]
    for i in range(2):
        place = core if i == 0 else 1 - core
        for j in range(4):
            at = pl.ds(pl.multiple_of(place * 32 + 8 * j, 8), 8)
            rows = q_ref[pl.ds(pl.multiple_of(chip * 64 + place * 32 + 8 * j, 8), 8), :]
            scores = dot_rows(rows, held[2 * i][512 * j : 512 * j + 512])
            lane = iota(scores.shape, 1)
            usable = (lane % 2 == core) & (lane < 2 * scalars[2 + 4 * i + j])
            scores = jnp.where(usable, scores, masked_score)
            highest = jnp.max(scores, axis=1, keepdims=True)
            weights = jnp.where(usable, jnp.exp2((scores - highest) * LEVEL), 0.0)
            total = jnp.sum(weights, axis=1, keepdims=True)
            mean_ref[at, :] = dot(weights.astype(bf16), held[2 * i + 1][512 * j : 512 * j + 512])
            total_ref[at, :] = jnp.broadcast_to(total, (8, 128))
            high_ref[at, :] = jnp.broadcast_to(highest * LEVEL, (8, 128))


def own_part(scalars, queries, leaves):
    shape = jax.ShapeDtypeStruct((64, 128), f32)
    sources = [flat(x) for x in leaves]
    return pl.pallas_call(
        own_kernel,
        out_shape=(shape, shape, shape),
        in_specs=[SMEM] + [VMEM] * 5,
        out_specs=(VMEM, VMEM, VMEM),
        compiler_params=pltpu.CompilerParams(vmem_limit_bytes=16 << 20),
        cost_estimate=pl.CostEstimate(flops=17_000_000, bytes_accessed=400_000, transcendentals=40_000),
        name="own_part",
    )(scalars, queries, *sources)


def merge_kernel(parts_ref, high_ref, total_ref, mean_ref, out_ref):
    head = parts_ref[:, 64, :].astype(f32)
    small = parts_ref[:, 65, :].astype(f32)
    levels = jnp.transpose(head + pltpu.roll(head, 64, 1) + small)[0:64]
    own_level = high_ref[:, 0:1]
    top = jnp.maximum(jnp.max(levels, axis=1, keepdims=True), own_level)
    factors = jnp.exp2(levels - top)
    own_factor = jnp.exp2(own_level - top)
    total = jnp.sum(factors, axis=1, keepdims=True) + own_factor * total_ref[:, 0:1]
    weighted = own_factor * mean_ref[...]
    for chip in range(CHIPS):
        weighted += factors[:, chip : chip + 1] * parts_ref[chip, 0:64].astype(f32)
    attended = (weighted / total).astype(bf16)
    target, source = iota((64, 64), 0), iota((64, 64), 1)
    moved = jnp.where((target % 8) * 8 + target // 8 == source, 1.0, 0.0).astype(bf16)
    by_head = dot(moved, attended).astype(bf16)
    line = jnp.concatenate([by_head[8 * h : 8 * h + 8] for h in range(HEADS)], axis=1)
    for chip in range(CHIPS):
        out_ref[chip] = line


def merged(parts, high, total, mean):
    return pl.pallas_call(
        merge_kernel,
        out_shape=jax.ShapeDtypeStruct((CHIPS, 8, HEADS * 128), bf16),
        in_specs=[VMEM] * 4,
        out_specs=VMEM,
        compiler_params=pltpu.CompilerParams(vmem_limit_bytes=16 << 20),
        cost_estimate=pl.CostEstimate(flops=4_000_000, bytes_accessed=700_000, transcendentals=2_000),
        name="merged",
    )(parts, high, total, mean)


TILE = 1792


def gate_up_kernel(core, near_ref, far_ref, gain_ref, far_gain_ref, gate, up, pair, out, held, scaled, result, sems, out_sems):
    rows, hidden = gate.shape[0], pair.shape[1]
    copies, sent = [], []
    for i, near in enumerate((gate, up)):
        for at in range(0, hidden, TILE):
            start = pl.multiple_of(core[0] * hidden + at, TILE)
            far = pair.at[i * rows : (i + 1) * rows, at : at + TILE]
            for k, source in enumerate((near.at[:, pl.ds(start, TILE)], far)):
                copies.append(pltpu.make_async_copy(source, held.at[2 * i + k, :, at : at + TILE], sems.at[len(copies)]))
    for copy in copies:
        copy.start()

    def send(span):
        sent.append(pltpu.make_async_copy(result.at[:, span], out.at[:, span], out_sems.at[len(sent)]))
        sent[-1].start()

    squares = jnp.zeros((128, 1), f32)
    for i, (ref, gain) in enumerate(((near_ref, gain_ref), (far_ref, far_gain_ref))):
        stream = ref[...]
        squares += jnp.sum(stream * stream, axis=1, keepdims=True)
        scaled[i] = (stream * gain[...]).astype(bf16)
    large = squares.astype(bf16).astype(f32)
    middle = (squares - large).astype(bf16).astype(f32)
    small = squares - large - middle
    lane = iota((128, 128), 1)
    shown = jnp.where(lane == 0, large, jnp.where(lane == 1, middle, jnp.where(lane == 2, small, 0.0)))
    result[:, 2 * hidden :] = shown.astype(bf16)
    send(slice(2 * hidden, 2 * hidden + 128))
    for i in range(2):
        for at in range(0, hidden, TILE):
            done = 2 * len(sent) - 2
            copies[done].wait()
            copies[done + 1].wait()
            product = dot(scaled[0], held[2 * i, :, at : at + TILE]) + dot(scaled[1], held[2 * i + 1, :, at : at + TILE])
            result[:, i * hidden + at : i * hidden + at + TILE] = product.astype(bf16)
            send(slice(i * hidden + at, i * hidden + at + TILE))
    for copy in sent:
        copy.wait()


def gate_up(core, stream, stream_far, gain, gain_far, gate, up, pair):
    hidden = pair.shape[1]
    count = 2 * (hidden // TILE)
    return pl.pallas_call(
        gate_up_kernel,
        out_shape=jax.ShapeDtypeStruct((128, 2 * hidden + 128), bf16),
        in_specs=[SMEM] + [VMEM] * 4 + [HBM] * 3,
        out_specs=HBM,
        scratch_shapes=[
            pltpu.VMEM((4, 256, hidden), bf16),
            pltpu.VMEM((2, 128, 256), bf16),
            pltpu.VMEM((128, 2 * hidden + 128), bf16),
            pltpu.SemaphoreType.DMA((2 * count,)),
            pltpu.SemaphoreType.DMA((count + 1,)),
        ],
        compiler_params=pltpu.CompilerParams(vmem_limit_bytes=60 << 20),
        cost_estimate=pl.CostEstimate(flops=940_000_000, bytes_accessed=9_400_000, transcendentals=0),
        name="gate_up",
    )(core, stream, stream_far, gain, gain_far, gate, up, pair)


def load_kernel(core, weight, far_ref, near_out, far_out, token, sems):
    half = pl.ds(pl.multiple_of(core[0] * near_out.shape[0], 512), near_out.shape[0])
    copies = [
        pltpu.make_async_copy(weight.at[half, :], near_out, sems.at[0]),
        pltpu.make_async_copy(far_ref, far_out, sems.at[1]),
    ]
    for copy in copies:
        copy.start()
    token[...] = jnp.zeros_like(token)
    for copy in copies:
        copy.wait()


def load_down(core, weight, far):
    shape = jax.ShapeDtypeStruct(far.shape, bf16)
    return pl.pallas_call(
        load_kernel,
        out_shape=(shape, shape, jax.ShapeDtypeStruct((8, 128), f32)),
        in_specs=[SMEM, HBM, HBM],
        out_specs=(VMEM, VMEM, VMEM),
        scratch_shapes=[pltpu.SemaphoreType.DMA((2,))],
        compiler_params=pltpu.CompilerParams(vmem_limit_bytes=55 << 20),
        cost_estimate=pl.CostEstimate(flops=0, bytes_accessed=7_400_000, transcendentals=0),
        name="load_down",
    )(core, weight, far)


def activation_kernel(parts_ref, token, out_ref):
    hidden = out_ref.shape[2]

    def summed(at, width):
        total = parts_ref[0, :, at : at + width].astype(f32)
        for chip in range(1, CHIPS):
            total += parts_ref[chip, :, at : at + width].astype(f32)
        return total

    lane = iota((8, 128), 1)
    squares = jnp.sum(jnp.where(lane < 3, summed(2 * hidden, 128), 0.0), axis=1, keepdims=True)
    inverse = lax.rsqrt(squares / D + norm_eps)
    for at in range(0, hidden, 512):
        gate = summed(at, 512) * inverse
        upward = summed(hidden + at, 512) * inverse
        act = (gate / (1.0 + jnp.exp(-gate)) * upward).astype(bf16)
        for chip in range(CHIPS):
            out_ref[chip, :, at : at + 512] = act


def activation(parts, token):
    hidden = (parts.shape[2] - 128) // 2
    return pl.pallas_call(
        activation_kernel,
        out_shape=jax.ShapeDtypeStruct((CHIPS, 8, hidden), bf16),
        in_specs=[VMEM, HBM],
        out_specs=VMEM,
        compiler_params=pltpu.CompilerParams(vmem_limit_bytes=16 << 20),
        cost_estimate=pl.CostEstimate(flops=2_000_000, bytes_accessed=2_800_000, transcendentals=30_000),
        name="activation",
    )(parts, token)


def down_kernel(core, act_ref, near, far, out_ref):
    out_ref[core[0]] = dot(act_ref[...], near[...]).astype(bf16)
    out_ref[1 - core[0]] = dot(act_ref[...], far[...]).astype(bf16)


def down(core, acts, near, far):
    return pl.pallas_call(
        down_kernel,
        out_shape=jax.ShapeDtypeStruct((2, 128, far.shape[1]), bf16),
        in_specs=[SMEM, VMEM, VMEM, VMEM],
        out_specs=VMEM,
        compiler_params=pltpu.CompilerParams(vmem_limit_bytes=16 << 20),
        cost_estimate=pl.CostEstimate(flops=470_000_000, bytes_accessed=4_700_000, transcendentals=0),
        name="down",
    )(core, acts, near, far)


def on_device(
    queries,
    root_keys,
    root_values,
    mid_keys,
    mid_values,
    leaf_keys,
    leaf_values,
    mid_length,
    leaf_length,
    branch_mid,
    residual,
    norm_gain,
    out_weight,
    gate_weight,
    up_weight,
    down_weight,
):
    core = lax.axis_index("core")
    other = 1 - core
    chip = lax.axis_index(PLANE)
    head_size = queries.shape[2]
    hidden = gate_weight.shape[1] // 2

    halves = queries.reshape(4, 2, HEADS, head_size).transpose(1, 0, 2, 3)
    sent = jnp.broadcast_to(halves[None], (CHIPS, *halves.shape)).reshape(32, 4, HEADS, head_size)
    core_only = core.reshape(1)
    shared = (mid_keys, mid_values, root_keys, root_values)
    sent, shared = lax.optimization_barrier((sent, shared))
    gathered = exchange(sent, NODE).reshape(128 * HEADS, head_size)
    shared_far = [swapped(x) for x in shared]
    roots = split_root(core_only, (*shared[2:], *shared_far[2:]))

    nodes = jnp.stack([2 * chip + core, 2 * chip + other])
    routing = branch_mid[:, 0]
    place = jnp.arange(128)
    earlier = (routing[None, :] == routing[:, None]) & (place[None, :] < place[:, None])
    rank = jnp.sum(earlier.astype(jnp.int32), axis=1)
    slot = jnp.where(routing == nodes[0], rank, jnp.where(routing == nodes[1], CAP + rank, -CAP * CAP))
    slots = (slot[:, None] * HEADS + jnp.arange(HEADS)[None, :]).reshape(-1)

    payload = shared_part(
        jnp.concatenate([core_only, mid_length[nodes]]),
        gathered,
        slots[:, None],
        slots[None, :],
        (*shared[:2], *shared_far[:2]),
        roots,
    )
    leaves = (leaf_keys, leaf_values)
    payload, leaves = lax.optimization_barrier((payload, leaves))
    leaves = (*leaves, *[swapped(x) for x in leaves])
    scalars = jnp.concatenate([jnp.stack([core, chip]), leaf_length, swapped(leaf_length)])
    parts = exchange(payload, PLANE)
    own = own_part(scalars, gathered, leaves)
    attended = merged(parts, *own)
    attended_near = exchange(attended, PLANE).reshape(128, HEADS * head_size)
    pair, down_sent = cut(core_only, attended, gate_weight, up_weight, down_weight)
    attended_near, pair, down_sent = lax.optimization_barrier((attended_near, pair, down_sent))
    gain_far = swapped(norm_gain)
    attended_far, pair = lax.optimization_barrier((swapped(attended_near), pair))
    pair_far = swapped(pair)
    half_rows = out_weight.shape[0] // 2
    projected = jnp.dot(
        attended_near,
        lax.dynamic_slice_in_dim(out_weight, core * half_rows, half_rows, 0),
        preferred_element_type=f32,
    ) + jnp.dot(
        attended_far,
        lax.dynamic_slice_in_dim(out_weight, other * half_rows, half_rows, 0),
        preferred_element_type=f32,
    )
    share = projected.astype(bf16)
    stream = residual.astype(f32) + share.astype(f32)
    for step in (1, 2, 3):
        stream += lax.ppermute(share, "mp", [(i, (i + step) % 4) for i in range(4)]).astype(f32)
    stream_far = swapped(stream)
    payload = gate_up(
        core_only, stream, stream_far, norm_gain[None], gain_far[None], gate_weight, up_weight, pair_far
    )
    payload, down_sent = lax.optimization_barrier((payload, down_sent))
    parts = exchange(payload.reshape(CHIPS, 8, -1), PLANE)
    own_down, far_down, token = load_down(core_only, down_weight, swapped(down_sent))
    acts = exchange(activation(parts, token), PLANE).reshape(128, hidden)
    blocks = down(core_only, acts, own_down, far_down).reshape(8, 32, -1)
    arrived = exchange(blocks, ("core", "mp"))
    rows = lax.dynamic_slice_in_dim(stream, lax.axis_index("mp") * 32, 32, 0)
    return (rows + jnp.sum(arrived.astype(f32), axis=0)).astype(bf16)


def solution(mesh):
    fine = Mesh(mesh.devices.reshape(4, 4, 2, 4), ("z", "x", "core", "mp"))
    in_specs = (
        P(NODE, "mp", None),
        P(NODE, "mp", None),
        P(NODE, "mp", None),
        P(NODE, None, "mp", None),
        P(NODE, None, "mp", None),
        P(NODE, None, "mp", None),
        P(NODE, None, "mp", None),
        P(),
        P(NODE),
        P(),
        P(None, NODE),
        P(NODE),
        P("mp", NODE),
        P(NODE, "mp"),
        P(NODE, "mp"),
        P("mp", NODE),
    )
    return jax.shard_map(
        on_device, mesh=fine, in_specs=in_specs, out_specs=P("mp", NODE), check_vma=False
    )
```

```python
import functools
import math

import jax
import jax.numpy as jnp
from jax import lax
from jax.experimental import pallas as pl
from jax.experimental.pallas import tpu as pltpu
from jax.sharding import Mesh
from jax.sharding import PartitionSpec as P

D = 8192
CAP = 8
masked_score = -1e30
norm_eps = 1e-05
bf16 = jnp.bfloat16
f32 = jnp.float32
PLANE = ("z", "x")
NODE = ("z", "x", "core")
SWAP = [(0, 1), (1, 0)]


def exchange(x, axes):
    return lax.all_to_all(x, axes, split_axis=0, concat_axis=0, tiled=True)


def swapped(x):
    return lax.ppermute(x, "core", SWAP)


VMEM = pl.BlockSpec(memory_space=pltpu.VMEM)
SMEM = pl.BlockSpec(memory_space=pltpu.SMEM)
HBM = pl.BlockSpec(memory_space=pltpu.HBM)
CHIPS = 16
HEADS = 8
LEVEL = 128**-0.5 * math.log2(math.e)


def dot_rows(a, b):
    return lax.dot_general(a, b, (((1,), (1,)), ((), ())), preferred_element_type=f32)


def dot(a, b):
    return lax.dot_general(a, b, (((1,), (0,)), ((), ())), preferred_element_type=f32)


def iota(shape, dim):
    return lax.broadcasted_iota(jnp.int32, shape, dim)


def cut_kernel(core, gate, up, down, pair_ref, down_ref, sems):
    rows, hidden = gate.shape[0], down_ref.shape[0]
    half = pl.ds(pl.multiple_of((1 - core[0]) * hidden, 512), hidden)
    copies = [
        pltpu.make_async_copy(gate.at[:, half], pair_ref.at[0:rows], sems.at[0]),
        pltpu.make_async_copy(up.at[:, half], pair_ref.at[rows : 2 * rows], sems.at[1]),
        pltpu.make_async_copy(down.at[half, :], down_ref, sems.at[2]),
    ]
    for copy in copies:
        copy.start()
    for copy in copies:
        copy.wait()


def cut(core, gate, up, down):
    hidden = gate.shape[1] // 2
    return pl.pallas_call(
        cut_kernel,
        out_shape=(
            jax.ShapeDtypeStruct((2 * gate.shape[0], hidden), bf16),
            jax.ShapeDtypeStruct((hidden, down.shape[1]), bf16),
        ),
        in_specs=[SMEM] + [HBM] * 3,
        out_specs=(VMEM, VMEM),
        scratch_shapes=[pltpu.SemaphoreType.DMA((3,))],
        compiler_params=pltpu.CompilerParams(vmem_limit_bytes=56 << 20),
        cost_estimate=pl.CostEstimate(flops=0, bytes_accessed=11_000_000, transcendentals=0),
        name="cut",
    )(core, gate, up, down)


def split_kernel(core, *refs):
    sources, out_ref = refs[:4], refs[4]
    order = jnp.where(2 * iota((128, 256), 0) + core[0] == iota((128, 256), 1), 1.0, 0.0).astype(bf16)
    for i, ref in enumerate(sources):
        for start in range(0, ref.shape[0], 512):
            pair = jnp.concatenate([ref[start : start + 256], ref[start + 256 : start + 512]], axis=1)
            moved = dot(order, pair).astype(bf16)
            out_ref[i, start // 2 : start // 2 + 128] = moved[:, 0:128]
            out_ref[i, start // 2 + 128 : start // 2 + 256] = moved[:, 128:256]


def split_root(core, roots):
    sources = [flat(x) for x in roots]
    return pl.pallas_call(
        split_kernel,
        out_shape=jax.ShapeDtypeStruct((4, sources[0].shape[0] // 2, 128), bf16),
        in_specs=[SMEM] + [VMEM] * 4,
        out_specs=VMEM,
        compiler_params=pltpu.CompilerParams(vmem_limit_bytes=16 << 20),
        cost_estimate=pl.CostEstimate(flops=70_000_000, bytes_accessed=1_600_000, transcendentals=0),
        name="split_root",
    )(core, *sources)


def shared_kernel(scalars, q_ref, column_ref, row_ref, *refs):
    mids, (split, out_ref) = refs[:4], refs[4:]
    core = scalars[0]
    count = q_ref.shape[0]
    queries = q_ref[...]
    one = jnp.where(row_ref[...] == iota((128, count), 0), 1.0, 0.0).astype(bf16)
    picked = dot(one, queries).astype(bf16)
    levels, means = [], []
    for i in range(2):
        scores = dot_rows(picked[64 * i : 64 * i + 64], mids[2 * i][...])
        lane = iota(scores.shape, 1)
        usable = (lane % 2 == core) & (lane < 2 * scalars[1 + i])
        scores = jnp.where(usable, scores, masked_score)
        highest = jnp.max(scores, axis=1, keepdims=True)
        weights = jnp.where(usable, jnp.exp2((scores - highest) * LEVEL), 0.0)
        total = jnp.sum(weights, axis=1, keepdims=True)
        weighted = dot(weights.astype(bf16), mids[2 * i + 1][...])
        levels.append(highest * LEVEL + jnp.log2(total))
        means.append(weighted / total)
    level = jnp.concatenate(levels)
    mean = jnp.concatenate(means)
    eye = iota((128, 128), 0) == iota((128, 128), 1)
    level_row = jnp.sum(jnp.where(eye, level, 0.0), axis=0, keepdims=True)
    first = mean.astype(bf16)
    second = (mean - first.astype(f32)).astype(bf16)
    step = 256
    lanes = iota((64, 128), 1)
    diagonal = (lanes % 64) == iota((64, 128), 0)
    for at in range(0, count, step):
        here = column_ref[at : at + step] == iota((step, 128), 1)
        chosen = jnp.where(here, 1.0, 0.0).astype(bf16)
        known = dot(chosen, first) + dot(chosen, second)
        known_level = jnp.max(jnp.where(here, level_row, masked_score), axis=1, keepdims=True)
        rows = q_ref[at : at + step]
        near = dot_rows(rows, split[0])
        far = dot_rows(rows, split[2])
        highest = jnp.maximum(
            jnp.max(near, axis=1, keepdims=True), jnp.max(far, axis=1, keepdims=True)
        )
        top = jnp.maximum(highest * LEVEL, known_level)
        near = jnp.exp2(near * LEVEL - top)
        far = jnp.exp2(far * LEVEL - top)
        factor = jnp.exp2(known_level - top)
        total = factor + jnp.sum(near, axis=1, keepdims=True) + jnp.sum(far, axis=1, keepdims=True)
        weighted = (
            known * factor
            + dot(near.astype(bf16), split[1])
            + dot(far.astype(bf16), split[3])
        )
        result = weighted / total
        reached = top + jnp.log2(total)
        for j in range(step // 64):
            chip = at // 64 + j
            out_ref[chip, 0:64] = result[64 * j : 64 * j + 64].astype(bf16)
            line = jnp.sum(
                jnp.where(diagonal, reached[64 * j : 64 * j + 64], 0.0), axis=0, keepdims=True
            )
            large = line.astype(bf16).astype(f32)
            middle = (line - large).astype(bf16).astype(f32)
            small = line - large - middle
            pair = jnp.where(iota((1, 128), 1) < 64, large, middle)
            both = jnp.where(iota((16, 128), 0) == 0, pair, small)
            out_ref[chip, 64:80] = both.astype(bf16)


def flat(x):
    return x.reshape(-1, 128)


def shared_part(scalars, queries, column, row, mids, roots):
    return pl.pallas_call(
        shared_kernel,
        out_shape=jax.ShapeDtypeStruct((CHIPS, 80, 128), bf16),
        in_specs=[SMEM] + [VMEM] * 8,
        out_specs=VMEM,
        compiler_params=pltpu.CompilerParams(vmem_limit_bytes=32 << 20),
        cost_estimate=pl.CostEstimate(flops=800_000_000, bytes_accessed=4_300_000, transcendentals=1_200_000),
        name="shared_part",
    )(scalars, queries, column, row, *[flat(x) for x in mids], roots)


def own_kernel(scalars, q_ref, *refs):
    held, (high_ref, total_ref, mean_ref) = refs[:4], refs[4:]
    core, chip = scalars[0], scalars[1]
    for i in range(2):
        place = core if i == 0 else 1 - core
        for j in range(4):
            at = pl.ds(pl.multiple_of(place * 32 + 8 * j, 8), 8)
            rows = q_ref[pl.ds(pl.multiple_of(chip * 64 + place * 32 + 8 * j, 8), 8), :]
            scores = dot_rows(rows, held[2 * i][512 * j : 512 * j + 512])
            lane = iota(scores.shape, 1)
            usable = (lane % 2 == core) & (lane < 2 * scalars[2 + 4 * i + j])
            scores = jnp.where(usable, scores, masked_score)
            highest = jnp.max(scores, axis=1, keepdims=True)
            weights = jnp.where(usable, jnp.exp2((scores - highest) * LEVEL), 0.0)
            total = jnp.sum(weights, axis=1, keepdims=True)
            mean_ref[at, :] = dot(weights.astype(bf16), held[2 * i + 1][512 * j : 512 * j + 512])
            total_ref[at, :] = jnp.broadcast_to(total, (8, 128))
            high_ref[at, :] = jnp.broadcast_to(highest * LEVEL, (8, 128))


def own_part(scalars, queries, leaves):
    shape = jax.ShapeDtypeStruct((64, 128), f32)
    sources = [flat(x) for x in leaves]
    return pl.pallas_call(
        own_kernel,
        out_shape=(shape, shape, shape),
        in_specs=[SMEM] + [VMEM] * 5,
        out_specs=(VMEM, VMEM, VMEM),
        compiler_params=pltpu.CompilerParams(vmem_limit_bytes=16 << 20),
        cost_estimate=pl.CostEstimate(flops=17_000_000, bytes_accessed=400_000, transcendentals=40_000),
        name="own_part",
    )(scalars, queries, *sources)


def merge_kernel(parts_ref, high_ref, total_ref, mean_ref, out_ref):
    head = parts_ref[:, 64, :].astype(f32)
    small = parts_ref[:, 65, :].astype(f32)
    levels = jnp.transpose(head + pltpu.roll(head, 64, 1) + small)[0:64]
    own_level = high_ref[:, 0:1]
    top = jnp.maximum(jnp.max(levels, axis=1, keepdims=True), own_level)
    factors = jnp.exp2(levels - top)
    own_factor = jnp.exp2(own_level - top)
    total = jnp.sum(factors, axis=1, keepdims=True) + own_factor * total_ref[:, 0:1]
    weighted = own_factor * mean_ref[...]
    for chip in range(CHIPS):
        weighted += factors[:, chip : chip + 1] * parts_ref[chip, 0:64].astype(f32)
    attended = (weighted / total).astype(bf16)
    target, source = iota((64, 64), 0), iota((64, 64), 1)
    moved = jnp.where((target % 8) * 8 + target // 8 == source, 1.0, 0.0).astype(bf16)
    by_head = dot(moved, attended).astype(bf16)
    line = jnp.concatenate([by_head[8 * h : 8 * h + 8] for h in range(HEADS)], axis=1)
    for chip in range(CHIPS):
        out_ref[chip] = line


def merged(parts, high, total, mean):
    return pl.pallas_call(
        merge_kernel,
        out_shape=jax.ShapeDtypeStruct((CHIPS, 8, HEADS * 128), bf16),
        in_specs=[VMEM] * 4,
        out_specs=VMEM,
        compiler_params=pltpu.CompilerParams(vmem_limit_bytes=16 << 20),
        cost_estimate=pl.CostEstimate(flops=4_000_000, bytes_accessed=700_000, transcendentals=2_000),
        name="merged",
    )(parts, high, total, mean)


TILE = 1792


def gate_up_kernel(core, near_ref, far_ref, gain_ref, far_gain_ref, gate, up, pair, out, held, scaled, result, sems, out_sems):
    rows, hidden = gate.shape[0], pair.shape[1]
    copies, sent = [], []
    for i, near in enumerate((gate, up)):
        for at in range(0, hidden, TILE):
            start = pl.multiple_of(core[0] * hidden + at, TILE)
            far = pair.at[i * rows : (i + 1) * rows, at : at + TILE]
            for k, source in enumerate((near.at[:, pl.ds(start, TILE)], far)):
                copies.append(pltpu.make_async_copy(source, held.at[2 * i + k, :, at : at + TILE], sems.at[len(copies)]))
    for copy in copies:
        copy.start()

    def send(span):
        sent.append(pltpu.make_async_copy(result.at[:, span], out.at[:, span], out_sems.at[len(sent)]))
        sent[-1].start()

    squares = jnp.zeros((128, 1), f32)
    for i, (ref, gain) in enumerate(((near_ref, gain_ref), (far_ref, far_gain_ref))):
        stream = ref[...]
        squares += jnp.sum(stream * stream, axis=1, keepdims=True)
        scaled[i] = (stream * gain[...]).astype(bf16)
    large = squares.astype(bf16).astype(f32)
    middle = (squares - large).astype(bf16).astype(f32)
    small = squares - large - middle
    lane = iota((128, 128), 1)
    shown = jnp.where(lane == 0, large, jnp.where(lane == 1, middle, jnp.where(lane == 2, small, 0.0)))
    result[:, 2 * hidden :] = shown.astype(bf16)
    send(slice(2 * hidden, 2 * hidden + 128))
    for i in range(2):
        for at in range(0, hidden, TILE):
            done = 2 * len(sent) - 2
            copies[done].wait()
            copies[done + 1].wait()
            product = dot(scaled[0], held[2 * i, :, at : at + TILE]) + dot(scaled[1], held[2 * i + 1, :, at : at + TILE])
            result[:, i * hidden + at : i * hidden + at + TILE] = product.astype(bf16)
            send(slice(i * hidden + at, i * hidden + at + TILE))
    for copy in sent:
        copy.wait()


def gate_up(core, stream, stream_far, gain, gain_far, gate, up, pair):
    hidden = pair.shape[1]
    count = 2 * (hidden // TILE)
    return pl.pallas_call(
        gate_up_kernel,
        out_shape=jax.ShapeDtypeStruct((128, 2 * hidden + 128), bf16),
        in_specs=[SMEM] + [VMEM] * 4 + [HBM] * 3,
        out_specs=HBM,
        scratch_shapes=[
            pltpu.VMEM((4, 256, hidden), bf16),
            pltpu.VMEM((2, 128, 256), bf16),
            pltpu.VMEM((128, 2 * hidden + 128), bf16),
            pltpu.SemaphoreType.DMA((2 * count,)),
            pltpu.SemaphoreType.DMA((count + 1,)),
        ],
        compiler_params=pltpu.CompilerParams(vmem_limit_bytes=60 << 20),
        cost_estimate=pl.CostEstimate(flops=940_000_000, bytes_accessed=9_400_000, transcendentals=0),
        name="gate_up",
    )(core, stream, stream_far, gain, gain_far, gate, up, pair)


def load_kernel(core, weight, far_ref, near_out, far_out, token, sems):
    half = pl.ds(pl.multiple_of(core[0] * near_out.shape[0], 512), near_out.shape[0])
    copies = [
        pltpu.make_async_copy(weight.at[half, :], near_out, sems.at[0]),
        pltpu.make_async_copy(far_ref, far_out, sems.at[1]),
    ]
    for copy in copies:
        copy.start()
    token[...] = jnp.zeros_like(token)
    for copy in copies:
        copy.wait()


def load_down(core, weight, far):
    shape = jax.ShapeDtypeStruct(far.shape, bf16)
    return pl.pallas_call(
        load_kernel,
        out_shape=(shape, shape, jax.ShapeDtypeStruct((8, 128), f32)),
        in_specs=[SMEM, HBM, HBM],
        out_specs=(VMEM, VMEM, VMEM),
        scratch_shapes=[pltpu.SemaphoreType.DMA((2,))],
        compiler_params=pltpu.CompilerParams(vmem_limit_bytes=55 << 20),
        cost_estimate=pl.CostEstimate(flops=0, bytes_accessed=7_400_000, transcendentals=0),
        name="load_down",
    )(core, weight, far)


def activation_kernel(parts_ref, token, out_ref):
    hidden = out_ref.shape[2]

    def summed(at, width):
        total = parts_ref[0, :, at : at + width].astype(f32)
        for chip in range(1, CHIPS):
            total += parts_ref[chip, :, at : at + width].astype(f32)
        return total

    lane = iota((8, 128), 1)
    squares = jnp.sum(jnp.where(lane < 3, summed(2 * hidden, 128), 0.0), axis=1, keepdims=True)
    inverse = lax.rsqrt(squares / D + norm_eps)
    for at in range(0, hidden, 512):
        gate = summed(at, 512) * inverse
        upward = summed(hidden + at, 512) * inverse
        act = (gate / (1.0 + jnp.exp(-gate)) * upward).astype(bf16)
        for chip in range(CHIPS):
            out_ref[chip, :, at : at + 512] = act


def activation(parts, token):
    hidden = (parts.shape[2] - 128) // 2
    return pl.pallas_call(
        activation_kernel,
        out_shape=jax.ShapeDtypeStruct((CHIPS, 8, hidden), bf16),
        in_specs=[VMEM, HBM],
        out_specs=VMEM,
        compiler_params=pltpu.CompilerParams(vmem_limit_bytes=16 << 20),
        cost_estimate=pl.CostEstimate(flops=2_000_000, bytes_accessed=2_800_000, transcendentals=30_000),
        name="activation",
    )(parts, token)


def down_kernel(core, act_ref, near, far, out_ref):
    out_ref[core[0]] = dot(act_ref[...], near[...]).astype(bf16)
    out_ref[1 - core[0]] = dot(act_ref[...], far[...]).astype(bf16)


def down(core, acts, near, far):
    return pl.pallas_call(
        down_kernel,
        out_shape=jax.ShapeDtypeStruct((2, 128, far.shape[1]), bf16),
        in_specs=[SMEM, VMEM, VMEM, VMEM],
        out_specs=VMEM,
        compiler_params=pltpu.CompilerParams(vmem_limit_bytes=16 << 20),
        cost_estimate=pl.CostEstimate(flops=470_000_000, bytes_accessed=4_700_000, transcendentals=0),
        name="down",
    )(core, acts, near, far)


def on_device(
    queries,
    root_keys,
    root_values,
    mid_keys,
    mid_values,
    leaf_keys,
    leaf_values,
    mid_length,
    leaf_length,
    branch_mid,
    residual,
    norm_gain,
    out_weight,
    gate_weight,
    up_weight,
    down_weight,
):
    core = lax.axis_index("core")
    other = 1 - core
    chip = lax.axis_index(PLANE)
    head_size = queries.shape[2]
    hidden = gate_weight.shape[1] // 2

    to_first = (jnp.arange(32) % 2 == 0)[:, None, None, None]
    sent = jnp.where(to_first, queries[None, :, :HEADS], queries[None, :, HEADS:])
    core_only = core.reshape(1)
    shared = (mid_keys, mid_values, root_keys, root_values)
    sent, shared = lax.optimization_barrier((sent, shared))
    gathered = exchange(sent, NODE).reshape(128 * HEADS, head_size)
    shared_far = [swapped(x) for x in shared]
    roots = split_root(core_only, (*shared[2:], *shared_far[2:]))

    nodes = jnp.stack([2 * chip + core, 2 * chip + other])
    routing = branch_mid[:, 0]
    place = jnp.arange(128)
    earlier = (routing[None, :] == routing[:, None]) & (place[None, :] < place[:, None])
    rank = jnp.sum(earlier.astype(jnp.int32), axis=1)
    slot = jnp.where(routing == nodes[0], rank, jnp.where(routing == nodes[1], CAP + rank, -CAP * CAP))
    slots = (slot[:, None] * HEADS + jnp.arange(HEADS)[None, :]).reshape(-1)

    payload = shared_part(
        jnp.concatenate([core_only, mid_length[nodes]]),
        gathered,
        slots[:, None],
        slots[None, :],
        (*shared[:2], *shared_far[:2]),
        roots,
    )
    leaves = (leaf_keys, leaf_values)
    payload, leaves = lax.optimization_barrier((payload, leaves))
    leaves = (*leaves, *[swapped(x) for x in leaves])
    scalars = jnp.concatenate([jnp.stack([core, chip]), leaf_length, swapped(leaf_length)])
    parts = exchange(payload, PLANE)
    own = own_part(scalars, gathered, leaves)
    attended = merged(parts, *own)
    attended_near = exchange(attended, PLANE).reshape(128, HEADS * head_size)
    pair, down_sent = cut(core_only, gate_weight, up_weight, down_weight)
    attended_near, pair, down_sent = lax.optimization_barrier((attended_near, pair, down_sent))
    gain_far = swapped(norm_gain)
    attended_far, pair = lax.optimization_barrier((swapped(attended_near), pair))
    pair_far = swapped(pair)
    half_rows = out_weight.shape[0] // 2
    projected = jnp.dot(
        attended_near,
        lax.dynamic_slice_in_dim(out_weight, core * half_rows, half_rows, 0),
        preferred_element_type=f32,
    ) + jnp.dot(
        attended_far,
        lax.dynamic_slice_in_dim(out_weight, other * half_rows, half_rows, 0),
        preferred_element_type=f32,
    )
    share = projected.astype(bf16)
    stream = residual.astype(f32) + share.astype(f32)
    for step in (1, 2, 3):
        stream += lax.ppermute(share, "mp", [(i, (i + step) % 4) for i in range(4)]).astype(f32)
    stream_far = swapped(stream)
    payload = gate_up(
        core_only, stream, stream_far, norm_gain[None], gain_far[None], gate_weight, up_weight, pair_far
    )
    stream_rows = lax.dynamic_slice_in_dim(stream, lax.axis_index("mp") * 32, 32, 0)
    payload, down_sent, stream_rows = lax.optimization_barrier((payload, down_sent, stream_rows))
    parts = exchange(payload.reshape(CHIPS, 8, -1), PLANE)
    own_down, far_down, token = load_down(core_only, down_weight, swapped(down_sent))
    acts = exchange(activation(parts, token), PLANE).reshape(128, hidden)
    blocks = down(core_only, acts, own_down, far_down).reshape(8, 32, -1)
    arrived = exchange(blocks, ("core", "mp"))
    return (stream_rows + jnp.sum(arrived.astype(f32), axis=0)).astype(bf16)


def solution(mesh):
    fine = Mesh(mesh.devices.reshape(4, 4, 2, 4), ("z", "x", "core", "mp"))
    in_specs = (
        P(NODE, "mp", None),
        P(NODE, "mp", None),
        P(NODE, "mp", None),
        P(NODE, None, "mp", None),
        P(NODE, None, "mp", None),
        P(NODE, None, "mp", None),
        P(NODE, None, "mp", None),
        P(),
        P(NODE),
        P(),
        P(None, NODE),
        P(NODE),
        P("mp", NODE),
        P(NODE, "mp"),
        P(NODE, "mp"),
        P("mp", NODE),
    )
    return jax.shard_map(
        on_device, mesh=fine, in_specs=in_specs, out_specs=P("mp", NODE), check_vma=False
    )
```

```python
import functools
import math

import jax
import jax.numpy as jnp
from jax import lax
from jax.experimental import pallas as pl
from jax.experimental.pallas import tpu as pltpu
from jax.sharding import Mesh
from jax.sharding import PartitionSpec as P

D = 8192
CAP = 8
masked_score = -1e30
norm_eps = 1e-05
bf16 = jnp.bfloat16
f32 = jnp.float32
PLANE = ("z", "x")
NODE = ("z", "x", "core")
SWAP = [(0, 1), (1, 0)]


def exchange(x, axes):
    return lax.all_to_all(x, axes, split_axis=0, concat_axis=0, tiled=True)


def swapped(x):
    return lax.ppermute(x, "core", SWAP)


VMEM = pl.BlockSpec(memory_space=pltpu.VMEM)
SMEM = pl.BlockSpec(memory_space=pltpu.SMEM)
HBM = pl.BlockSpec(memory_space=pltpu.HBM)
CHIPS = 16
HEADS = 8
LEVEL = 128**-0.5 * math.log2(math.e)


def dot_rows(a, b):
    return lax.dot_general(a, b, (((1,), (1,)), ((), ())), preferred_element_type=f32)


def dot(a, b):
    return lax.dot_general(a, b, (((1,), (0,)), ((), ())), preferred_element_type=f32)


def iota(shape, dim):
    return lax.broadcasted_iota(jnp.int32, shape, dim)


def cut_kernel(core, gate, up, down, pair_ref, down_ref, sems):
    rows, hidden = gate.shape[0], down_ref.shape[0]
    half = pl.ds(pl.multiple_of((1 - core[0]) * hidden, 512), hidden)
    copies = [
        pltpu.make_async_copy(gate.at[:, half], pair_ref.at[0:rows], sems.at[0]),
        pltpu.make_async_copy(up.at[:, half], pair_ref.at[rows : 2 * rows], sems.at[1]),
        pltpu.make_async_copy(down.at[half, :], down_ref, sems.at[2]),
    ]
    for copy in copies:
        copy.start()
    for copy in copies:
        copy.wait()


def cut(core, gate, up, down):
    hidden = gate.shape[1] // 2
    return pl.pallas_call(
        cut_kernel,
        out_shape=(
            jax.ShapeDtypeStruct((2 * gate.shape[0], hidden), bf16),
            jax.ShapeDtypeStruct((hidden, down.shape[1]), bf16),
        ),
        in_specs=[SMEM] + [HBM] * 3,
        out_specs=(VMEM, VMEM),
        scratch_shapes=[pltpu.SemaphoreType.DMA((3,))],
        compiler_params=pltpu.CompilerParams(vmem_limit_bytes=56 << 20),
        cost_estimate=pl.CostEstimate(flops=0, bytes_accessed=11_000_000, transcendentals=0),
        name="cut",
    )(core, gate, up, down)


def split_kernel(core, *refs):
    sources, out_ref = refs[:4], refs[4]
    order = jnp.where(2 * iota((128, 256), 0) + core[0] == iota((128, 256), 1), 1.0, 0.0).astype(bf16)
    for i, ref in enumerate(sources):
        for start in range(0, ref.shape[0], 512):
            pair = jnp.concatenate([ref[start : start + 256], ref[start + 256 : start + 512]], axis=1)
            moved = dot(order, pair).astype(bf16)
            out_ref[i, start // 2 : start // 2 + 128] = moved[:, 0:128]
            out_ref[i, start // 2 + 128 : start // 2 + 256] = moved[:, 128:256]


def split_root(core, roots):
    sources = [flat(x) for x in roots]
    return pl.pallas_call(
        split_kernel,
        out_shape=jax.ShapeDtypeStruct((4, sources[0].shape[0] // 2, 128), bf16),
        in_specs=[SMEM] + [VMEM] * 4,
        out_specs=VMEM,
        compiler_params=pltpu.CompilerParams(vmem_limit_bytes=16 << 20),
        cost_estimate=pl.CostEstimate(flops=70_000_000, bytes_accessed=1_600_000, transcendentals=0),
        name="split_root",
    )(core, *sources)


def shared_kernel(scalars, q_ref, column_ref, row_ref, *refs):
    mids, (split, out_ref) = refs[:4], refs[4:]
    core = scalars[0]
    count = q_ref.shape[0]
    queries = q_ref[...]
    one = jnp.where(row_ref[...] == iota((128, count), 0), 1.0, 0.0).astype(bf16)
    picked = dot(one, queries).astype(bf16)
    levels, means = [], []
    for i in range(2):
        scores = dot_rows(picked[64 * i : 64 * i + 64], mids[2 * i][...])
        lane = iota(scores.shape, 1)
        usable = (lane % 2 == core) & (lane < 2 * scalars[1 + i])
        scores = jnp.where(usable, scores, masked_score)
        highest = jnp.max(scores, axis=1, keepdims=True)
        weights = jnp.where(usable, jnp.exp2((scores - highest) * LEVEL), 0.0)
        total = jnp.sum(weights, axis=1, keepdims=True)
        weighted = dot(weights.astype(bf16), mids[2 * i + 1][...])
        levels.append(highest * LEVEL + jnp.log2(total))
        means.append(weighted / total)
    level = jnp.concatenate(levels)
    mean = jnp.concatenate(means)
    eye = iota((128, 128), 0) == iota((128, 128), 1)
    level_row = jnp.sum(jnp.where(eye, level, 0.0), axis=0, keepdims=True)
    first = mean.astype(bf16)
    second = (mean - first.astype(f32)).astype(bf16)
    step = 512
    lanes = iota((64, 128), 1)
    diagonal = (lanes % 64) == iota((64, 128), 0)
    for at in range(0, count, step):
        here = column_ref[at : at + step] == iota((step, 128), 1)
        chosen = jnp.where(here, 1.0, 0.0).astype(bf16)
        known = dot(chosen, first) + dot(chosen, second)
        known_level = jnp.max(jnp.where(here, level_row, masked_score), axis=1, keepdims=True)
        rows = q_ref[at : at + step]
        near = dot_rows(rows, split[0])
        far = dot_rows(rows, split[2])
        highest = jnp.maximum(
            jnp.max(near, axis=1, keepdims=True), jnp.max(far, axis=1, keepdims=True)
        )
        top = jnp.maximum(highest * LEVEL, known_level)
        near = jnp.exp2(near * LEVEL - top)
        far = jnp.exp2(far * LEVEL - top)
        factor = jnp.exp2(known_level - top)
        total = factor + jnp.sum(near, axis=1, keepdims=True) + jnp.sum(far, axis=1, keepdims=True)
        weighted = (
            known * factor
            + dot(near.astype(bf16), split[1])
            + dot(far.astype(bf16), split[3])
        )
        result = weighted / total
        reached = top + jnp.log2(total)
        for j in range(step // 64):
            chip = at // 64 + j
            out_ref[chip, 0:64] = result[64 * j : 64 * j + 64].astype(bf16)
            line = jnp.sum(
                jnp.where(diagonal, reached[64 * j : 64 * j + 64], 0.0), axis=0, keepdims=True
            )
            large = line.astype(bf16).astype(f32)
            middle = (line - large).astype(bf16).astype(f32)
            small = line - large - middle
            pair = jnp.where(iota((1, 128), 1) < 64, large, middle)
            both = jnp.where(iota((16, 128), 0) == 0, pair, small)
            out_ref[chip, 64:80] = both.astype(bf16)


def flat(x):
    return x.reshape(-1, 128)


def shared_part(scalars, queries, column, row, mids, roots):
    return pl.pallas_call(
        shared_kernel,
        out_shape=jax.ShapeDtypeStruct((CHIPS, 80, 128), bf16),
        in_specs=[SMEM] + [VMEM] * 8,
        out_specs=VMEM,
        compiler_params=pltpu.CompilerParams(vmem_limit_bytes=32 << 20),
        cost_estimate=pl.CostEstimate(flops=800_000_000, bytes_accessed=4_300_000, transcendentals=1_200_000),
        name="shared_part",
    )(scalars, queries, column, row, *[flat(x) for x in mids], roots)


def own_kernel(scalars, q_ref, *refs):
    held, (high_ref, total_ref, mean_ref) = refs[:4], refs[4:]
    core, chip = scalars[0], scalars[1]
    for i in range(2):
        place = core if i == 0 else 1 - core
        for j in range(4):
            at = pl.ds(pl.multiple_of(place * 32 + 8 * j, 8), 8)
            rows = q_ref[pl.ds(pl.multiple_of(chip * 64 + place * 32 + 8 * j, 8), 8), :]
            scores = dot_rows(rows, held[2 * i][512 * j : 512 * j + 512])
            lane = iota(scores.shape, 1)
            usable = (lane % 2 == core) & (lane < 2 * scalars[2 + 4 * i + j])
            scores = jnp.where(usable, scores, masked_score)
            highest = jnp.max(scores, axis=1, keepdims=True)
            weights = jnp.where(usable, jnp.exp2((scores - highest) * LEVEL), 0.0)
            total = jnp.sum(weights, axis=1, keepdims=True)
            mean_ref[at, :] = dot(weights.astype(bf16), held[2 * i + 1][512 * j : 512 * j + 512])
            total_ref[at, :] = jnp.broadcast_to(total, (8, 128))
            high_ref[at, :] = jnp.broadcast_to(highest * LEVEL, (8, 128))


def own_part(scalars, queries, leaves):
    shape = jax.ShapeDtypeStruct((64, 128), f32)
    sources = [flat(x) for x in leaves]
    return pl.pallas_call(
        own_kernel,
        out_shape=(shape, shape, shape),
        in_specs=[SMEM] + [VMEM] * 5,
        out_specs=(VMEM, VMEM, VMEM),
        compiler_params=pltpu.CompilerParams(vmem_limit_bytes=16 << 20),
        cost_estimate=pl.CostEstimate(flops=17_000_000, bytes_accessed=400_000, transcendentals=40_000),
        name="own_part",
    )(scalars, queries, *sources)


def merge_kernel(parts_ref, high_ref, total_ref, mean_ref, out_ref):
    head = parts_ref[:, 64, :].astype(f32)
    small = parts_ref[:, 65, :].astype(f32)
    levels = jnp.transpose(head + pltpu.roll(head, 64, 1) + small)[0:64]
    own_level = high_ref[:, 0:1]
    top = jnp.maximum(jnp.max(levels, axis=1, keepdims=True), own_level)
    factors = jnp.exp2(levels - top)
    own_factor = jnp.exp2(own_level - top)
    total = jnp.sum(factors, axis=1, keepdims=True) + own_factor * total_ref[:, 0:1]
    weighted = own_factor * mean_ref[...]
    for chip in range(CHIPS):
        weighted += factors[:, chip : chip + 1] * parts_ref[chip, 0:64].astype(f32)
    attended = (weighted / total).astype(bf16)
    target, source = iota((64, 64), 0), iota((64, 64), 1)
    moved = jnp.where((target % 8) * 8 + target // 8 == source, 1.0, 0.0).astype(bf16)
    by_head = dot(moved, attended).astype(bf16)
    line = jnp.concatenate([by_head[8 * h : 8 * h + 8] for h in range(HEADS)], axis=1)
    for chip in range(CHIPS):
        out_ref[chip] = line


def merged(parts, high, total, mean):
    return pl.pallas_call(
        merge_kernel,
        out_shape=jax.ShapeDtypeStruct((CHIPS, 8, HEADS * 128), bf16),
        in_specs=[VMEM] * 4,
        out_specs=VMEM,
        compiler_params=pltpu.CompilerParams(vmem_limit_bytes=16 << 20),
        cost_estimate=pl.CostEstimate(flops=4_000_000, bytes_accessed=700_000, transcendentals=2_000),
        name="merged",
    )(parts, high, total, mean)


TILE = 896


def gate_up_kernel(core, near_ref, far_ref, gain_ref, far_gain_ref, gate, up, pair, out, held, scaled, result, sems, out_sems):
    rows, hidden = gate.shape[0], pair.shape[1]
    copies, sent = [], []
    for i, near in enumerate((gate, up)):
        for at in range(0, hidden, TILE):
            start = pl.multiple_of(core[0] * hidden + at, TILE)
            far = pair.at[i * rows : (i + 1) * rows, at : at + TILE]
            for k, source in enumerate((near.at[:, pl.ds(start, TILE)], far)):
                copies.append(pltpu.make_async_copy(source, held.at[2 * i + k, :, at : at + TILE], sems.at[len(copies)]))
    for copy in copies:
        copy.start()

    def send(span):
        sent.append(pltpu.make_async_copy(result.at[:, span], out.at[:, span], out_sems.at[len(sent)]))
        sent[-1].start()

    squares = jnp.zeros((128, 1), f32)
    for i, (ref, gain) in enumerate(((near_ref, gain_ref), (far_ref, far_gain_ref))):
        stream = ref[...]
        squares += jnp.sum(stream * stream, axis=1, keepdims=True)
        scaled[i] = (stream * gain[...]).astype(bf16)
    large = squares.astype(bf16).astype(f32)
    middle = (squares - large).astype(bf16).astype(f32)
    small = squares - large - middle
    lane = iota((128, 128), 1)
    shown = jnp.where(lane == 0, large, jnp.where(lane == 1, middle, jnp.where(lane == 2, small, 0.0)))
    result[:, 2 * hidden :] = shown.astype(bf16)
    send(slice(2 * hidden, 2 * hidden + 128))
    for i in range(2):
        for at in range(0, hidden, TILE):
            done = 2 * len(sent) - 2
            copies[done].wait()
            copies[done + 1].wait()
            product = dot(scaled[0], held[2 * i, :, at : at + TILE]) + dot(scaled[1], held[2 * i + 1, :, at : at + TILE])
            result[:, i * hidden + at : i * hidden + at + TILE] = product.astype(bf16)
            send(slice(i * hidden + at, i * hidden + at + TILE))
    for copy in sent:
        copy.wait()


def gate_up(core, stream, stream_far, gain, gain_far, gate, up, pair):
    hidden = pair.shape[1]
    count = 2 * (hidden // TILE)
    return pl.pallas_call(
        gate_up_kernel,
        out_shape=jax.ShapeDtypeStruct((128, 2 * hidden + 128), bf16),
        in_specs=[SMEM] + [VMEM] * 4 + [HBM] * 3,
        out_specs=HBM,
        scratch_shapes=[
            pltpu.VMEM((4, 256, hidden), bf16),
            pltpu.VMEM((2, 128, 256), bf16),
            pltpu.VMEM((128, 2 * hidden + 128), bf16),
            pltpu.SemaphoreType.DMA((2 * count,)),
            pltpu.SemaphoreType.DMA((count + 1,)),
        ],
        compiler_params=pltpu.CompilerParams(vmem_limit_bytes=60 << 20),
        cost_estimate=pl.CostEstimate(flops=940_000_000, bytes_accessed=9_400_000, transcendentals=0),
        name="gate_up",
    )(core, stream, stream_far, gain, gain_far, gate, up, pair)


def load_kernel(core, weight, far_ref, near_out, far_out, token, sems):
    half = pl.ds(pl.multiple_of(core[0] * near_out.shape[0], 512), near_out.shape[0])
    copies = [
        pltpu.make_async_copy(weight.at[half, :], near_out, sems.at[0]),
        pltpu.make_async_copy(far_ref, far_out, sems.at[1]),
    ]
    for copy in copies:
        copy.start()
    token[...] = jnp.zeros_like(token)
    for copy in copies:
        copy.wait()


def load_down(core, weight, far):
    shape = jax.ShapeDtypeStruct(far.shape, bf16)
    return pl.pallas_call(
        load_kernel,
        out_shape=(shape, shape, jax.ShapeDtypeStruct((8, 128), f32)),
        in_specs=[SMEM, HBM, HBM],
        out_specs=(VMEM, VMEM, VMEM),
        scratch_shapes=[pltpu.SemaphoreType.DMA((2,))],
        compiler_params=pltpu.CompilerParams(vmem_limit_bytes=55 << 20),
        cost_estimate=pl.CostEstimate(flops=0, bytes_accessed=7_400_000, transcendentals=0),
        name="load_down",
    )(core, weight, far)


def activation_kernel(parts_ref, token, out_ref):
    hidden = out_ref.shape[2]

    def summed(at, width):
        total = parts_ref[0, :, at : at + width].astype(f32)
        for chip in range(1, CHIPS):
            total += parts_ref[chip, :, at : at + width].astype(f32)
        return total

    lane = iota((8, 128), 1)
    squares = jnp.sum(jnp.where(lane < 3, summed(2 * hidden, 128), 0.0), axis=1, keepdims=True)
    inverse = lax.rsqrt(squares / D + norm_eps)
    for at in range(0, hidden, 512):
        gate = summed(at, 512) * inverse
        upward = summed(hidden + at, 512) * inverse
        act = (gate / (1.0 + jnp.exp(-gate)) * upward).astype(bf16)
        for chip in range(CHIPS):
            out_ref[chip, :, at : at + 512] = act


def activation(parts, token):
    hidden = (parts.shape[2] - 128) // 2
    return pl.pallas_call(
        activation_kernel,
        out_shape=jax.ShapeDtypeStruct((CHIPS, 8, hidden), bf16),
        in_specs=[VMEM, HBM],
        out_specs=VMEM,
        compiler_params=pltpu.CompilerParams(vmem_limit_bytes=16 << 20),
        cost_estimate=pl.CostEstimate(flops=2_000_000, bytes_accessed=2_800_000, transcendentals=30_000),
        name="activation",
    )(parts, token)


def down_kernel(core, act_ref, near, far, out_ref):
    out_ref[core[0]] = dot(act_ref[...], near[...]).astype(bf16)
    out_ref[1 - core[0]] = dot(act_ref[...], far[...]).astype(bf16)


def down(core, acts, near, far):
    return pl.pallas_call(
        down_kernel,
        out_shape=jax.ShapeDtypeStruct((2, 128, far.shape[1]), bf16),
        in_specs=[SMEM, VMEM, VMEM, VMEM],
        out_specs=VMEM,
        compiler_params=pltpu.CompilerParams(vmem_limit_bytes=16 << 20),
        cost_estimate=pl.CostEstimate(flops=470_000_000, bytes_accessed=4_700_000, transcendentals=0),
        name="down",
    )(core, acts, near, far)


def on_device(
    queries,
    root_keys,
    root_values,
    mid_keys,
    mid_values,
    leaf_keys,
    leaf_values,
    mid_length,
    leaf_length,
    branch_mid,
    residual,
    norm_gain,
    out_weight,
    gate_weight,
    up_weight,
    down_weight,
):
    core = lax.axis_index("core")
    other = 1 - core
    chip = lax.axis_index(PLANE)
    head_size = queries.shape[2]
    hidden = gate_weight.shape[1] // 2

    to_first = (jnp.arange(32) % 2 == 0)[:, None, None, None]
    sent = jnp.where(to_first, queries[None, :, :HEADS], queries[None, :, HEADS:])
    core_only = core.reshape(1)
    shared = (mid_keys, mid_values, root_keys, root_values)
    sent, shared = lax.optimization_barrier((sent, shared))
    gathered = exchange(sent, NODE).reshape(128 * HEADS, head_size)
    shared_far = [swapped(x) for x in shared]
    roots = split_root(core_only, (*shared[2:], *shared_far[2:]))

    nodes = jnp.stack([2 * chip + core, 2 * chip + other])
    routing = branch_mid[:, 0]
    place = jnp.arange(128)
    earlier = (routing[None, :] == routing[:, None]) & (place[None, :] < place[:, None])
    rank = jnp.sum(earlier.astype(jnp.int32), axis=1)
    slot = jnp.where(routing == nodes[0], rank, jnp.where(routing == nodes[1], CAP + rank, -CAP * CAP))
    slots = (slot[:, None] * HEADS + jnp.arange(HEADS)[None, :]).reshape(-1)

    payload = shared_part(
        jnp.concatenate([core_only, mid_length[nodes]]),
        gathered,
        slots[:, None],
        slots[None, :],
        (*shared[:2], *shared_far[:2]),
        roots,
    )
    leaves = (leaf_keys, leaf_values)
    payload, leaves = lax.optimization_barrier((payload, leaves))
    leaves = (*leaves, *[swapped(x) for x in leaves])
    scalars = jnp.concatenate([jnp.stack([core, chip]), leaf_length, swapped(leaf_length)])
    parts = exchange(payload, PLANE)
    own = own_part(scalars, gathered, leaves)
    attended = merged(parts, *own)
    attended_near = exchange(attended, PLANE).reshape(128, HEADS * head_size)
    pair, down_sent = cut(core_only, gate_weight, up_weight, down_weight)
    attended_near, pair, down_sent = lax.optimization_barrier((attended_near, pair, down_sent))
    gain_far = swapped(norm_gain)
    attended_far, pair = lax.optimization_barrier((swapped(attended_near), pair))
    pair_far = swapped(pair)
    half_rows = out_weight.shape[0] // 2
    projected = jnp.dot(
        attended_near,
        lax.dynamic_slice_in_dim(out_weight, core * half_rows, half_rows, 0),
        preferred_element_type=f32,
    ) + jnp.dot(
        attended_far,
        lax.dynamic_slice_in_dim(out_weight, other * half_rows, half_rows, 0),
        preferred_element_type=f32,
    )
    share = projected.astype(bf16)
    stream = residual.astype(f32) + share.astype(f32)
    for step in (1, 2, 3):
        stream += lax.ppermute(share, "mp", [(i, (i + step) % 4) for i in range(4)]).astype(f32)
    stream_far = swapped(stream)
    payload = gate_up(
        core_only, stream, stream_far, norm_gain[None], gain_far[None], gate_weight, up_weight, pair_far
    )
    stream_rows = lax.dynamic_slice_in_dim(stream, lax.axis_index("mp") * 32, 32, 0)
    payload, down_sent, stream_rows = lax.optimization_barrier((payload, down_sent, stream_rows))
    parts = exchange(payload.reshape(CHIPS, 8, -1), PLANE)
    own_down, far_down, token = load_down(core_only, down_weight, swapped(down_sent))
    acts = exchange(activation(parts, token), PLANE).reshape(128, hidden)
    blocks = down(core_only, acts, own_down, far_down).reshape(8, 32, -1)
    arrived = exchange(blocks, ("core", "mp"))
    return (stream_rows + jnp.sum(arrived.astype(f32), axis=0)).astype(bf16)


def solution(mesh):
    fine = Mesh(mesh.devices.reshape(4, 4, 2, 4), ("z", "x", "core", "mp"))
    in_specs = (
        P(NODE, "mp", None),
        P(NODE, "mp", None),
        P(NODE, "mp", None),
        P(NODE, None, "mp", None),
        P(NODE, None, "mp", None),
        P(NODE, None, "mp", None),
        P(NODE, None, "mp", None),
        P(),
        P(NODE),
        P(),
        P(None, NODE),
        P(NODE),
        P("mp", NODE),
        P(NODE, "mp"),
        P(NODE, "mp"),
        P("mp", NODE),
    )
    return jax.shard_map(
        on_device, mesh=fine, in_specs=in_specs, out_specs=P("mp", NODE), check_vma=False
    )
```
